32 devices in a mesh: row: 4 (over y, x), col: 8 (over z, core).
Axes of the slice: x: 2, y: 2, z: 4, core: 2. Of those that a mesh axis runs over, the one named last changes fastest.
Arguments:
- out_grad: bfloat16 [4096, 8192], P('row', 'col'), may hold values from -0.059814453 to 0.059814453
- hidden: bfloat16 [4096, 28672], P('row', 'col'), may hold values from -6 to 6
- basis: bfloat16 [8192, 1024], P('col'), may hold values from -0.0625 to 0.0625
- weight: bfloat16 [8192, 28672], P('row', 'col'), may hold values from -6 to 6
- first_moment: float32 [1024, 28672], P('row', 'col'), may hold values from -4 to 4
- second_moment: float32 [1024, 28672], P('row', 'col'), may hold values from 0.25 to 4
Outputs:
- new_weight: bfloat16 [8192, 28672], P('row', 'col')
- new_first: float32 [1024, 28672], P('row', 'col')
- new_second: float32 [1024, 28672], P('row', 'col')
The draws below stay inside these ranges and needn't reach their ends.
All inputs are finite; a program needn't handle non-finite values.
Results may differ from the reference program's by a relative error of at most 0.0039.
Values may be sent and summed in bfloat16 or wider, within the bound.
A program may use at most 128 MiB of HBM per device.

```python
import math
import jax
import jax.numpy as jnp

D = 8192
FF = 28672
RANK = 1024
STEP_COUNT = 1000
TOKENS = 4096


def levels(own_key, shape, pieces, smallest, top_value):
    def one(position, shards_of):
        heights = jax.random.uniform(jax.random.fold_in(jax.random.fold_in(own_key, 6), position), (shards_of,), jnp.float32, smallest / len(pieces), top_value / len(pieces))
        return jnp.repeat(jnp.exp(heights), shape[position] // shards_of).reshape((-1,) + (1,) * (len(shape) - position - 1))

    loudness = one(*pieces[0])
    for cut in pieces[1:]:
        loudness = loudness * one(*cut)
    return loudness


def normal_values(key, dims, scale, reach, shards=(), dtype=jnp.bfloat16):
    drawn = scale * jax.random.normal(key, dims, jnp.float32)
    if shards:
        drawn = drawn * levels(key, dims, shards, -0.22, 0.18)
    return jnp.clip(drawn, -reach, reach).astype(dtype)


def setup_inputs(seed: int = 0) -> dict:
    key_of = jax.random.split(jax.random.key(seed), 7)
    return {
        "out_grad": normal_values(key_of[0], (TOKENS, D), 0.01, 0.059814453, ((0, 4), (1, 8))),
        "hidden": normal_values(key_of[1], (TOKENS, FF), 1.0, 6.0, ((0, 4), (1, 8))),
        "basis": normal_values(key_of[2], (D, RANK), D ** -0.5, 0.0625, ((0, 8),)),
        "weight": normal_values(key_of[3], (D, FF), 1.0, 6.0, ((0, 4), (1, 8))),
        "first_moment": normal_values(key_of[4], (RANK, FF), 0.5, 4.0, ((0, 4), (1, 8)), jnp.float32),
        "second_moment": jnp.clip(jnp.exp(math.log(4.0) - 2.7725887 * jax.random.uniform(key_of[5], (RANK, FF), jnp.float32) ** levels(key_of[5], (RANK, FF), ((0, 4), (1, 8)), -0.2, 0.2)), 0.25, 4.0),
    }


beta_one = 0.9
beta_two = 0.999
epsilon = 1e-08
step_size = 1.0

def reference(out_grad, hidden, basis, weight, first_moment, second_moment):
    projected = jnp.dot(out_grad, basis, preferred_element_type=jnp.float32).astype(jnp.bfloat16)
    gradient = jnp.dot(projected.T, hidden, preferred_element_type=jnp.float32)
    new_first = beta_one * first_moment + (1.0 - beta_one) * gradient
    new_second = beta_two * second_moment + (1.0 - beta_two) * gradient * gradient
    first_hat = new_first / (1.0 - beta_one ** STEP_COUNT)
    second_hat = new_second / (1.0 - beta_two ** STEP_COUNT)
    direction = (first_hat / (jnp.sqrt(second_hat) + epsilon)).astype(jnp.bfloat16)
    update = jnp.dot(basis, direction, preferred_element_type=jnp.float32)
    new_weight = (weight.astype(jnp.float32) - step_size * update).astype(jnp.bfloat16)
    return (new_weight, new_first, new_second)
```

```python
import functools

import jax
import jax.numpy as jnp
from jax import lax
from jax.experimental import pallas as pl
from jax.experimental.pallas import tpu as pltpu
from jax.sharding import PartitionSpec as P

STEP_COUNT = 1000


beta_one = 0.9
beta_two = 0.999
epsilon = 1e-08
step_size = 1.0

MESH = pl.DeviceIdType.MESH


def row_kernel(
    A, B, steps, rb, W,
    proj, hidden, first, second,
    gathered, new_first, new_second,
    hid, par, one_b, one_a, mid_b, mid_a, two_b, two_a, gat, mom_one, mom_two,
    load, out_sem,
    s1b, r1b, s1a, r1a, s2b, r2b, s2a, r2a,
    sgb, rgb, sga, rga, srb, rrb, sra, rra,
):
    row = lax.axis_index("row")
    a, b = row // B, lax.rem(row, B)

    def to_a(k):
        return {"row": lax.rem(a + k, A) * B + b}

    def to_b(k):
        return {"row": a * B + lax.rem(b + k, B)}

    def span(s):
        return pl.ds(pl.multiple_of(s * 2 * W, 2 * W), 2 * W)

    def loads(s):
        return (
            pltpu.make_async_copy(hidden.at[:, span(s)], hid.at[s], load.at[0, s]),
            pltpu.make_async_copy(first.at[:, span(s)], mom_one.at[s], load.at[1, s]),
            pltpu.make_async_copy(second.at[:, span(s)], mom_two.at[s], load.at[2, s]),
        )

    def stores(s):
        return (
            pltpu.make_async_copy(mom_one.at[s], new_first.at[:, span(s)], out_sem.at[1, s]),
            pltpu.make_async_copy(mom_two.at[s], new_second.at[:, span(s)], out_sem.at[2, s]),
        )

    def remote(src, dst, send, recv, device):
        return pltpu.make_async_remote_copy(
            src_ref=src, dst_ref=dst, send_sem=send, recv_sem=recv,
            device_id=device, device_id_type=MESH,
        )

    def first_hops(s):
        for k in range(1, B):
            yield remote(par.at[s, 0, :, lax.rem(b + k, B)], one_b.at[s, k - 1],
                         s1b.at[s, k - 1], r1b.at[s, k - 1], to_b(k))
        for k in range(1, A):
            yield remote(par.at[s, 1, lax.rem(a + k, A)], one_a.at[s, k - 1],
                         s1a.at[s, k - 1], r1a.at[s, k - 1], to_a(k))

    def second_hops(s):
        for k in range(1, A):
            yield remote(mid_b.at[s, lax.rem(a + k, A)], two_b.at[s, k - 1],
                         s2b.at[s, k - 1], r2b.at[s, k - 1], to_a(k))
        for k in range(1, B):
            yield remote(mid_a.at[s, lax.rem(b + k, B)], two_a.at[s, k - 1],
                         s2a.at[s, k - 1], r2a.at[s, k - 1], to_b(k))

    def own_sends(s):
        for k in range(1, B):
            yield remote(gat.at[s, :, a, b], gat.at[s, :, a, b],
                         sgb.at[s, k - 1], rgb.at[s, k - 1], to_b(k))
        for k in range(1, A):
            yield remote(gat.at[s, :, a, b], gat.at[s, :, a, b],
                         sga.at[s, k - 1], rga.at[s, k - 1], to_a(k))

    def relays(s):
        for j in range(1, B):
            for k in range(1, A):
                block = gat.at[s, 0, a, lax.rem(b + j, B)]
                i = (j - 1) * (A - 1) + k - 1
                yield remote(block, block, srb.at[s, i], rrb.at[s, i], to_a(k))
        for j in range(1, A):
            for k in range(1, B):
                block = gat.at[s, 1, lax.rem(a + j, A), b]
                i = (j - 1) * (B - 1) + k - 1
                yield remote(block, block, sra.at[s, i], rra.at[s, i], to_b(k))

    def result(s):
        return pltpu.make_async_copy(gat.at[s], gathered.at[s], out_sem.at[0, s])

    def every(body):
        lax.fori_loop(0, steps, lambda s, c: (body(s), c)[1], 0)

    every(lambda s: [c.start() for c in loads(s)])

    barrier = pltpu.get_barrier_semaphore()
    for k in range(1, B):
        pl.semaphore_signal(barrier, inc=1, device_id=to_b(k), device_id_type=MESH)
    for k in range(1, A):
        pl.semaphore_signal(barrier, inc=1, device_id=to_a(k), device_id_type=MESH)
    pl.semaphore_wait(barrier, A + B - 2)

    f32 = jnp.float32

    def turn(it, carry):
        @pl.when(it < steps)
        def _():
            s = it
            loads(s)[0].wait()
            for t in range(2):
                got = jnp.dot(proj[...], hid[s, :, t * W:(t + 1) * W],
                              preferred_element_type=f32)
                par[s, t] = got.astype(jnp.bfloat16).reshape(A, B, rb, W)
            for c in first_hops(s):
                c.start()

        @pl.when((it >= 1) & (it < steps + 1))
        def _():
            s = it - 1
            for c in first_hops(s):
                c.wait_recv()
            for i in range(A):
                total = par[s, 0, i, b].astype(f32)
                for k in range(B - 1):
                    total += one_b[s, k, i].astype(f32)
                mid_b[s, i] = total.astype(jnp.bfloat16)
            for i in range(B):
                total = par[s, 1, a, i].astype(f32)
                for k in range(A - 1):
                    total += one_a[s, k, i].astype(f32)
                mid_a[s, i] = total.astype(jnp.bfloat16)
            for c in second_hops(s):
                c.start()

        @pl.when((it >= 2) & (it < steps + 2))
        def _():
            s = it - 2
            for c in second_hops(s):
                c.wait_recv()
            for c in loads(s)[1:]:
                c.wait()
            for t in range(2):
                if t == 0:
                    gradient = mid_b[s, a].astype(f32)
                    for k in range(A - 1):
                        gradient += two_b[s, k].astype(f32)
                else:
                    gradient = mid_a[s, b].astype(f32)
                    for k in range(B - 1):
                        gradient += two_a[s, k].astype(f32)
                cols = slice(t * W, (t + 1) * W)
                one = beta_one * mom_one[s, :, cols] + (1.0 - beta_one) * gradient
                two = beta_two * mom_two[s, :, cols] + (1.0 - beta_two) * gradient * gradient
                first_hat = one / (1.0 - beta_one**STEP_COUNT)
                second_hat = two / (1.0 - beta_two**STEP_COUNT)
                gat[s, t, a, b] = (first_hat / (jnp.sqrt(second_hat) + epsilon)).astype(jnp.bfloat16)
                mom_one[s, :, cols] = one
                mom_two[s, :, cols] = two
            for c in own_sends(s):
                c.start()
            for c in stores(s):
                c.start()

        @pl.when((it >= 3) & (it < steps + 3))
        def _():
            s = it - 3
            for c in own_sends(s):
                c.wait_recv()
            for c in relays(s):
                c.start()

        @pl.when(it >= 4)
        def _():
            s = it - 4
            for c in relays(s):
                c.wait_recv()
            result(s).start()

        return carry

    lax.fori_loop(0, steps + 4, turn, 0)

    def finish(s):
        for group in (first_hops, second_hops, own_sends, relays):
            for c in group(s):
                c.wait_send()
        for c in stores(s):
            c.wait()
        result(s).wait()

    every(finish)


def row_part(rows, proj, hidden, first, second):
    B = 2 if rows % 2 == 0 else 1
    A = rows // B
    rank, tokens = proj.shape
    rb, cols = first.shape
    W = 256 if cols % 512 == 0 else 128
    steps = cols // (2 * W)
    bf16, f32 = jnp.bfloat16, jnp.float32
    nb, na = max(B - 1, 1), max(A - 1, 1)
    nr = na * nb

    def pair(n):
        return [pltpu.SemaphoreType.DMA((steps, n)), pltpu.SemaphoreType.DMA((steps, n))]

    anywhere = pl.BlockSpec(memory_space=pl.ANY)
    return pl.pallas_call(
        functools.partial(row_kernel, A, B, steps, rb, W),
        name="row_part",
        out_shape=(
            jax.ShapeDtypeStruct((steps, 2, A, B, rb, W), bf16),
            jax.ShapeDtypeStruct(first.shape, f32),
            jax.ShapeDtypeStruct(second.shape, f32),
        ),
        in_specs=[pl.BlockSpec(memory_space=pltpu.VMEM), anywhere, anywhere, anywhere],
        out_specs=(anywhere, anywhere, anywhere),
        scratch_shapes=[
            pltpu.VMEM((steps, tokens, 2 * W), bf16),
            pltpu.VMEM((steps, 2, A, B, rb, W), bf16),
            pltpu.VMEM((steps, nb, A, rb, W), bf16),
            pltpu.VMEM((steps, na, B, rb, W), bf16),
            pltpu.VMEM((steps, A, rb, W), bf16),
            pltpu.VMEM((steps, B, rb, W), bf16),
            pltpu.VMEM((steps, na, rb, W), bf16),
            pltpu.VMEM((steps, nb, rb, W), bf16),
            pltpu.VMEM((steps, 2, A, B, rb, W), bf16),
            pltpu.VMEM((steps, rb, 2 * W), f32),
            pltpu.VMEM((steps, rb, 2 * W), f32),
            pltpu.SemaphoreType.DMA((3, steps)),
            pltpu.SemaphoreType.DMA((3, steps)),
        ] + pair(nb) + pair(na) + pair(na) + pair(nb) + pair(nb) + pair(na) + pair(nr) + pair(nr),
        compiler_params=pltpu.CompilerParams(
            collective_id=0, has_side_effects=True, vmem_limit_bytes=60 << 20
        ),
        cost_estimate=pl.CostEstimate(
            flops=2 * rank * tokens * cols * 8, bytes_accessed=400 << 20, transcendentals=0
        ),
    )(proj, hidden, first, second)


def update_kernel(W, which, basis, direction, weight, out):
    for t in range(2):
        cols = slice(t * W, (t + 1) * W)
        update = jnp.dot(basis[...], direction[0, t], preferred_element_type=jnp.float32)
        out[:, cols] = (weight[:, cols].astype(jnp.float32) - step_size * update).astype(jnp.bfloat16)


def apply_update(index, basis, gathered, weight):
    steps, _, rank, W = gathered.shape
    rows, cols = weight.shape
    wide = pl.BlockSpec((rows, 2 * W), lambda j, r: (0, j))
    return pl.pallas_call(
        functools.partial(update_kernel, W),
        name="apply_update",
        out_shape=jax.ShapeDtypeStruct(weight.shape, weight.dtype),
        grid_spec=pltpu.PrefetchScalarGridSpec(
            num_scalar_prefetch=1,
            grid=(steps,),
            in_specs=[
                pl.BlockSpec((rows, rank), lambda j, r: (r[0], 0), pipeline_mode=pl.Buffered(1)),
                pl.BlockSpec((1, 2, rank, W), lambda j, r: (j, 0, 0, 0)),
                wide,
            ],
            out_specs=wide,
        ),
        compiler_params=pltpu.CompilerParams(
            dimension_semantics=("arbitrary",), vmem_limit_bytes=56 << 20
        ),
        cost_estimate=pl.CostEstimate(
            flops=2 * rank * rows * cols, bytes_accessed=3 * weight.size * 2, transcendentals=0
        ),
    )(index, basis, gathered, weight)


def local(rows, out_grad, hidden, basis, weight, first_moment, second_moment):
    part = lax.dot_general(
        basis, out_grad, (((0,), (1,)), ((), ())), preferred_element_type=jnp.float32
    ).astype(jnp.bfloat16)
    proj = lax.psum_scatter(part, "col", scatter_dimension=0, tiled=True)
    proj = lax.all_gather(proj, "col", axis=0, tiled=True)
    late, proj = lax.optimization_barrier((basis, proj))
    whole = lax.all_gather(late, "col", axis=0, tiled=True)
    gathered, new_first, new_second = row_part(rows, proj, hidden, first_moment, second_moment)
    steps, W = gathered.shape[0], gathered.shape[-1]
    gathered = gathered.reshape(steps, 2, -1, W)
    index = lax.axis_index("row").astype(jnp.int32).reshape(1)
    new_weight = apply_update(index, whole, gathered, weight)
    return (new_weight, new_first, new_second)


def solution(mesh):
    in_specs = (
        P("row", "col"),
        P("row", "col"),
        P("col", None),
        P("row", "col"),
        P("row", "col"),
        P("row", "col"),
    )
    out_specs = (P("row", "col"), P("row", "col"), P("row", "col"))
    return jax.shard_map(
        functools.partial(local, mesh.shape["row"]),
        mesh=mesh, in_specs=in_specs, out_specs=out_specs, check_vma=False,
    )
```

```python
import functools

import jax
import jax.numpy as jnp
from jax import lax
from jax.experimental import pallas as pl
from jax.experimental.pallas import tpu as pltpu
from jax.sharding import PartitionSpec as P

STEP_COUNT = 1000


beta_one = 0.9
beta_two = 0.999
epsilon = 1e-08
step_size = 1.0

MESH = pl.DeviceIdType.MESH


def row_kernel(
    A, B, Z, steps, rb, W, chunks,
    part, hidden, first, second, basis,
    gathered, new_first, new_second, spread,
    cross, chip, terms, proj, bas,
    hid, par, one_b, one_a, mid_b, mid_a, two_b, two_a, gat, mom_one, mom_two,
    load, out_sem,
    s1b, r1b, s1a, r1a, s2b, r2b, s2a, r2a,
    sgb, rgb, sga, rga, srb, rrb, sra, rra,
    scx, rcx, szr, rzr, szg, rzg, spg, rpg,
    sbu, sbd, rbc, sbp, rbp, bas_in, bas_out,
):
    row = lax.axis_index("row")
    a, b = row // B, lax.rem(row, B)
    col = lax.axis_index("col")
    z, core = col // 2, lax.rem(col, 2)
    partner = {"col": z * 2 + 1 - core}
    pieces = sorted(
        [(i, j) for i in range(A) for j in range(B)],
        key=lambda d: -(d[0] > 0) - (d[1] > 0),
    )

    def to_z(k):
        return {"col": lax.rem(z + k, Z) * 2 + core}

    def to_a(k):
        return {"row": lax.rem(a + k, A) * B + b}

    def to_b(k):
        return {"row": a * B + lax.rem(b + k, B)}

    def span(s):
        return pl.ds(pl.multiple_of(s * 2 * W, 2 * W), 2 * W)

    def loads(s):
        return (
            pltpu.make_async_copy(hidden.at[:, span(s)], hid.at[s], load.at[0, s]),
            pltpu.make_async_copy(first.at[:, span(s)], mom_one.at[s], load.at[1, s]),
            pltpu.make_async_copy(second.at[:, span(s)], mom_two.at[s], load.at[2, s]),
        )

    def stores(s):
        return (
            pltpu.make_async_copy(mom_one.at[s], new_first.at[:, span(s)], out_sem.at[1, s]),
            pltpu.make_async_copy(mom_two.at[s], new_second.at[:, span(s)], out_sem.at[2, s]),
        )

    def remote(src, dst, send, recv, device):
        return pltpu.make_async_remote_copy(
            src_ref=src, dst_ref=dst, send_sem=send, recv_sem=recv,
            device_id=device, device_id_type=MESH,
        )

    def first_hop(s, da, db):
        i, j = lax.rem(a + da, A), lax.rem(b + db, B)
        if db:
            n = (db - 1) * A + da
            yield remote(par.at[s, 0, i, j], one_b.at[s, db - 1, i],
                         s1b.at[s, n], r1b.at[s, n], to_b(db))
        if da:
            n = (da - 1) * B + db
            yield remote(par.at[s, 1, i, j], one_a.at[s, da - 1, j],
                         s1a.at[s, n], r1a.at[s, n], to_a(da))

    def first_hops(s):
        for piece in pieces:
            yield from first_hop(s, *piece)

    def second_hops(s):
        for k in range(1, A):
            yield remote(mid_b.at[s, lax.rem(a + k, A)], two_b.at[s, k - 1],
                         s2b.at[s, k - 1], r2b.at[s, k - 1], to_a(k))
        for k in range(1, B):
            yield remote(mid_a.at[s, lax.rem(b + k, B)], two_a.at[s, k - 1],
                         s2a.at[s, k - 1], r2a.at[s, k - 1], to_b(k))

    def own_sends(s):
        for k in range(1, B):
            yield remote(gat.at[s, :, a, b], gat.at[s, :, a, b],
                         sgb.at[s, k - 1], rgb.at[s, k - 1], to_b(k))
        for k in range(1, A):
            yield remote(gat.at[s, :, a, b], gat.at[s, :, a, b],
                         sga.at[s, k - 1], rga.at[s, k - 1], to_a(k))

    def relays(s):
        for j in range(1, B):
            for k in range(1, A):
                block = gat.at[s, 0, a, lax.rem(b + j, B)]
                i = (j - 1) * (A - 1) + k - 1
                yield remote(block, block, srb.at[s, i], rrb.at[s, i], to_a(k))
        for j in range(1, A):
            for k in range(1, B):
                block = gat.at[s, 1, lax.rem(a + j, A), b]
                i = (j - 1) * (B - 1) + k - 1
                yield remote(block, block, sra.at[s, i], rra.at[s, i], to_b(k))

    def block_of(p):
        return lax.rem(a + pieces[p][0], A), lax.rem(b + pieces[p][1], B)

    def crossing(p):
        i, j = block_of(p)
        yield remote(part.at[i, j, 1 - core], cross.at[p], scx.at[p], rcx.at[p], partner)

    def scatters(p):
        for k in range(1, Z):
            yield remote(chip.at[p, lax.rem(z + k, Z)], terms.at[p, k - 1],
                         szr.at[p, k - 1], rzr.at[p, k - 1], to_z(k))

    def gathers(p):
        i, j = block_of(p)
        block = proj.at[i, j, core, z]
        for k in range(1, Z):
            yield remote(block, block, szg.at[p, k - 1], rzg.at[p, k - 1], to_z(k))

    def shares(p, first_k, last_k):
        i, j = block_of(p)
        for k in range(first_k, last_k):
            block = proj.at[i, j, core, lax.rem(z + k, Z)]
            yield remote(block, block, spg.at[p, k], rpg.at[p, k], partner)

    source = row
    far = jnp.abs(z - source)

    def upward(i):
        block = bas.at[core, i]
        return remote(block, block, sbu.at[i], rbc.at[i], {"col": lax.rem(z + 1, Z) * 2 + core})

    def downward(i):
        block = bas.at[core, i]
        return remote(block, block, sbd.at[i], rbc.at[i], {"col": lax.rem(z + Z - 1, Z) * 2 + core})

    def beside(i):
        block = bas.at[core, i]
        return remote(block, block, sbp.at[i], rbp.at[i], partner)

    goes_up = (z >= source) & (z < Z - 1)
    goes_down = (z <= source) & (z > 0)

    def spread_step(it):
        i = it - far

        @pl.when((i >= 0) & (i < chunks))
        def _():
            @pl.when(far > 0)
            def _():
                upward(i).wait_recv()

            @pl.when(goes_up)
            def _():
                upward(i).start()

            @pl.when(goes_down)
            def _():
                downward(i).start()

            beside(i).start()

    def result(s):
        return pltpu.make_async_copy(gat.at[s], gathered.at[s], out_sem.at[0, s])

    def every(body):
        lax.fori_loop(0, steps, lambda s, c: (body(s), c)[1], 0)

    own_basis = pltpu.make_async_copy(basis, bas.at[core], bas_in)

    @pl.when(far == 0)
    def _():
        own_basis.start()

    every(lambda s: [c.start() for c in loads(s)])

    barrier = pltpu.get_barrier_semaphore()
    for k in range(1, B):
        pl.semaphore_signal(barrier, inc=1, device_id=to_b(k), device_id_type=MESH)
    for k in range(1, A):
        pl.semaphore_signal(barrier, inc=1, device_id=to_a(k), device_id_type=MESH)
    for k in range(1, Z):
        pl.semaphore_signal(barrier, inc=1, device_id=to_z(k), device_id_type=MESH)
    pl.semaphore_signal(barrier, inc=1, device_id=partner, device_id_type=MESH)
    pl.semaphore_wait(barrier, A + B + Z - 2)

    f32, bf16 = jnp.float32, jnp.bfloat16
    count = len(pieces)
    for p in range(count):
        for c in crossing(p):
            c.start()
    for it in range(count + 3):
        p = it
        if 0 <= p < count:
            i, j = block_of(p)
            for c in crossing(p):
                c.wait_recv()
            chip[p] = (part[i, j, core].astype(f32) + cross[p].astype(f32)).astype(bf16)
            for c in scatters(p):
                c.start()
        p = it - 1
        if 0 <= p < count:
            i, j = block_of(p)
            for c in scatters(p):
                c.wait_recv()
            total = chip[p, z].astype(f32)
            for k in range(Z - 1):
                total += terms[p, k].astype(f32)
            proj[i, j, core, z] = total.astype(bf16)
            for c in gathers(p):
                c.start()
            for c in shares(p, 0, 1):
                c.start()
        p = it - 2
        if 0 <= p < count:
            for c in gathers(p):
                c.wait_recv()
            for c in shares(p, 1, Z):
                c.start()
        p = it - 3
        if 0 <= p < count:
            i, j = block_of(p)
            for c in shares(p, 0, Z):
                c.wait_recv()

            def partial_step(s, carry, p=p, i=i, j=j):
                if p == 0:
                    loads(s)[0].wait()
                got = jnp.dot(proj[i, j].reshape(rb, -1), hid[s], preferred_element_type=f32)
                par[s, 0, i, j] = got[:, :W].astype(bf16)
                par[s, 1, i, j] = got[:, W:].astype(bf16)
                for c in first_hop(s, *pieces[p]):
                    c.start()
                return carry

            lax.fori_loop(0, steps, partial_step, 0)

    @pl.when(far == 0)
    def _():
        own_basis.wait()

    def turn(it, carry):
        spread_step(it)

        @pl.when(it < steps)
        def _():
            s = it
            for c in first_hops(s):
                c.wait_recv()
            for i in range(A):
                total = par[s, 0, i, b].astype(f32)
                for k in range(B - 1):
                    total += one_b[s, k, i].astype(f32)
                mid_b[s, i] = total.astype(jnp.bfloat16)
            for i in range(B):
                total = par[s, 1, a, i].astype(f32)
                for k in range(A - 1):
                    total += one_a[s, k, i].astype(f32)
                mid_a[s, i] = total.astype(jnp.bfloat16)
            for c in second_hops(s):
                c.start()

        @pl.when((it >= 1) & (it < steps + 1))
        def _():
            s = it - 1
            for c in second_hops(s):
                c.wait_recv()
            for c in loads(s)[1:]:
                c.wait()
            for t in range(2):
                if t == 0:
                    gradient = mid_b[s, a].astype(f32)
                    for k in range(A - 1):
                        gradient += two_b[s, k].astype(f32)
                else:
                    gradient = mid_a[s, b].astype(f32)
                    for k in range(B - 1):
                        gradient += two_a[s, k].astype(f32)
                cols = slice(t * W, (t + 1) * W)
                one = beta_one * mom_one[s, :, cols] + (1.0 - beta_one) * gradient
                two = beta_two * mom_two[s, :, cols] + (1.0 - beta_two) * gradient * gradient
                first_hat = one / (1.0 - beta_one**STEP_COUNT)
                second_hat = two / (1.0 - beta_two**STEP_COUNT)
                gat[s, t, a, b] = (first_hat / (jnp.sqrt(second_hat) + epsilon)).astype(jnp.bfloat16)
                mom_one[s, :, cols] = one
                mom_two[s, :, cols] = two
            for c in own_sends(s):
                c.start()
            for c in stores(s):
                c.start()

        @pl.when((it >= 2) & (it < steps + 2))
        def _():
            s = it - 2
            for c in own_sends(s):
                c.wait_recv()
            for c in relays(s):
                c.start()

        @pl.when((it >= 3) & (it < steps + 3))
        def _():
            s = it - 3
            for c in relays(s):
                c.wait_recv()
            result(s).start()

        return carry

    lax.fori_loop(0, max(steps + 3, chunks + Z - 1), turn, 0)

    def finish_basis(i, carry):
        beside(i).wait()

        @pl.when(goes_up)
        def _():
            upward(i).wait_send()

        @pl.when(goes_down)
        def _():
            downward(i).wait_send()

        return carry

    lax.fori_loop(0, chunks, finish_basis, 0)
    spread_out = pltpu.make_async_copy(bas, spread, bas_out)
    spread_out.start()
    for p in range(count):
        for group in (crossing(p), scatters(p), gathers(p), shares(p, 0, Z)):
            for c in group:
                c.wait_send()

    def finish(s):
        for group in (first_hops, second_hops, own_sends, relays):
            for c in group(s):
                c.wait_send()
        for c in stores(s):
            c.wait()
        result(s).wait()

    every(finish)
    spread_out.wait()


def row_part(rows, banks, part, hidden, first, second, basis):
    Z = banks // 2
    B = 2 if rows % 2 == 0 else 1
    A = rows // B
    rank, tokens = part.shape
    rb, cols = first.shape
    rk = rb // banks
    count = rows
    chunks = 8
    depth = basis.shape[0] // chunks
    part = part.reshape(A, B, 2, Z, rk, tokens)
    basis = basis.reshape(chunks, depth, rank)
    W = 256 if cols % 512 == 0 else 128
    steps = cols // (2 * W)
    bf16, f32 = jnp.bfloat16, jnp.float32
    nb, na = max(B - 1, 1), max(A - 1, 1)
    nr = na * nb

    def pair(n):
        return [pltpu.SemaphoreType.DMA((steps, n)), pltpu.SemaphoreType.DMA((steps, n))]

    def two(*shape):
        return [pltpu.SemaphoreType.DMA(shape), pltpu.SemaphoreType.DMA(shape)]

    one = pltpu.SemaphoreType.DMA((chunks,))

    anywhere = pl.BlockSpec(memory_space=pl.ANY)
    return pl.pallas_call(
        functools.partial(row_kernel, A, B, Z, steps, rb, W, chunks),
        name="row_part",
        out_shape=(
            jax.ShapeDtypeStruct((steps, 2, A, B, rb, W), bf16),
            jax.ShapeDtypeStruct(first.shape, f32),
            jax.ShapeDtypeStruct(second.shape, f32),
            jax.ShapeDtypeStruct((2,) + basis.shape, bf16),
        ),
        in_specs=[pl.BlockSpec(memory_space=pltpu.VMEM)] + [anywhere] * 4,
        out_specs=(anywhere,) * 4,
        scratch_shapes=[
            pltpu.VMEM((count, Z, rk, tokens), bf16),
            pltpu.VMEM((count, Z, rk, tokens), bf16),
            pltpu.VMEM((count, Z - 1, rk, tokens), bf16),
            pltpu.VMEM((A, B, 2, Z, rk, tokens), bf16),
            pltpu.VMEM((2,) + basis.shape, bf16),
            pltpu.VMEM((steps, tokens, 2 * W), bf16),
            pltpu.VMEM((steps, 2, A, B, rb, W), bf16),
            pltpu.VMEM((steps, nb, A, rb, W), bf16),
            pltpu.VMEM((steps, na, B, rb, W), bf16),
            pltpu.VMEM((steps, A, rb, W), bf16),
            pltpu.VMEM((steps, B, rb, W), bf16),
            pltpu.VMEM((steps, na, rb, W), bf16),
            pltpu.VMEM((steps, nb, rb, W), bf16),
            pltpu.VMEM((steps, 2, A, B, rb, W), bf16),
            pltpu.VMEM((steps, rb, 2 * W), f32),
            pltpu.VMEM((steps, rb, 2 * W), f32),
            pltpu.SemaphoreType.DMA((3, steps)),
            pltpu.SemaphoreType.DMA((3, steps)),
        ] + pair(nb * A) + pair(na * B) + pair(na) + pair(nb) + pair(nb) + pair(na) + pair(nr) + pair(nr)
        + two(count) + two(count, Z - 1) + two(count, Z - 1) + two(count, Z)
        + [one] * 5 + [pltpu.SemaphoreType.DMA, pltpu.SemaphoreType.DMA],
        compiler_params=pltpu.CompilerParams(
            collective_id=0, has_side_effects=True, vmem_limit_bytes=60 << 20
        ),
        cost_estimate=pl.CostEstimate(
            flops=2 * rank * tokens * cols * 8, bytes_accessed=400 << 20, transcendentals=0
        ),
    )(part, hidden, first, second, basis)


def update_kernel(W, basis, direction, weight, out):
    for t in range(2):
        cols = slice(t * W, (t + 1) * W)
        update = jnp.dot(basis[...], direction[0, t], preferred_element_type=jnp.float32)
        out[:, cols] = (weight[:, cols].astype(jnp.float32) - step_size * update).astype(jnp.bfloat16)


def apply_update(basis, gathered, weight):
    steps, _, rank, W = gathered.shape
    rows, cols = weight.shape
    wide = pl.BlockSpec((rows, 2 * W), lambda j: (0, j))
    return pl.pallas_call(
        functools.partial(update_kernel, W),
        name="apply_update",
        out_shape=jax.ShapeDtypeStruct(weight.shape, weight.dtype),
        grid=(steps,),
        in_specs=[
            pl.BlockSpec((rows, rank), lambda j: (0, 0), pipeline_mode=pl.Buffered(1)),
            pl.BlockSpec((1, 2, rank, W), lambda j: (j, 0, 0, 0)),
            wide,
        ],
        out_specs=wide,
        compiler_params=pltpu.CompilerParams(
            dimension_semantics=("arbitrary",), vmem_limit_bytes=56 << 20
        ),
        cost_estimate=pl.CostEstimate(
            flops=2 * rank * rows * cols, bytes_accessed=3 * weight.size * 2, transcendentals=0
        ),
    )(basis, gathered, weight)


def local(rows, banks, out_grad, hidden, basis, weight, first_moment, second_moment):
    part = lax.dot_general(
        basis, out_grad, (((0,), (1,)), ((), ())), preferred_element_type=jnp.float32
    ).astype(jnp.bfloat16)
    gathered, new_first, new_second, spread = row_part(
        rows, banks, part, hidden, first_moment, second_moment, basis
    )
    steps, W = gathered.shape[0], gathered.shape[-1]
    gathered = gathered.reshape(steps, 2, -1, W)
    new_weight = apply_update(spread.reshape(-1, basis.shape[1]), gathered, weight)
    return (new_weight, new_first, new_second)


def solution(mesh):
    in_specs = (
        P("row", "col"),
        P("row", "col"),
        P("col", None),
        P("row", "col"),
        P("row", "col"),
        P("row", "col"),
    )
    out_specs = (P("row", "col"), P("row", "col"), P("row", "col"))
    return jax.shard_map(
        functools.partial(local, mesh.shape["row"], mesh.shape["col"]),
        mesh=mesh, in_specs=in_specs, out_specs=out_specs, check_vma=False,
    )
```

```python
import functools

import jax
import jax.numpy as jnp
from jax import lax
from jax.experimental import pallas as pl
from jax.experimental.pallas import tpu as pltpu
from jax.sharding import PartitionSpec as P

STEP_COUNT = 1000


beta_one = 0.9
beta_two = 0.999
epsilon = 1e-08
step_size = 1.0

MESH = pl.DeviceIdType.MESH


def row_kernel(
    A, B, Z, steps, rb, W, chunks,
    part, hidden, first, second, basis,
    gathered, new_first, new_second, spread,
    cross, chip, terms, proj, bas,
    hid, par, one_b, one_a, mid_b, mid_a, two_b, two_a, gat, mom_one, mom_two,
    load, out_sem,
    s1b, r1b, s1a, r1a, s2b, r2b, s2a, r2a,
    sgb, rgb, sga, rga, srb, rrb, sra, rra,
    scx, rcx, szr, rzr, szg, rzg, spg, rpg,
    sbu, sbd, rbc, sbp, rbp, bas_in, bas_out,
):
    row = lax.axis_index("row")
    a, b = row // B, lax.rem(row, B)
    col = lax.axis_index("col")
    z, core = col // 2, lax.rem(col, 2)
    partner = {"col": z * 2 + 1 - core}
    pieces = sorted(
        [(i, j) for i in range(A) for j in range(B)],
        key=lambda d: -(d[0] > 0) - (d[1] > 0),
    )

    def to_z(k):
        return {"col": lax.rem(z + k, Z) * 2 + core}

    def to_a(k):
        return {"row": lax.rem(a + k, A) * B + b}

    def to_b(k):
        return {"row": a * B + lax.rem(b + k, B)}

    def span(s):
        return pl.ds(pl.multiple_of(s * 2 * W, 2 * W), 2 * W)

    def loads(s):
        return (
            pltpu.make_async_copy(hidden.at[:, span(s)], hid.at[s], load.at[0, s]),
            pltpu.make_async_copy(first.at[:, span(s)], mom_one.at[s], load.at[1, s]),
            pltpu.make_async_copy(second.at[:, span(s)], mom_two.at[s], load.at[2, s]),
        )

    def stores(s):
        return (
            pltpu.make_async_copy(mom_one.at[s], new_first.at[:, span(s)], out_sem.at[1, s]),
            pltpu.make_async_copy(mom_two.at[s], new_second.at[:, span(s)], out_sem.at[2, s]),
        )

    def remote(src, dst, send, recv, device):
        return pltpu.make_async_remote_copy(
            src_ref=src, dst_ref=dst, send_sem=send, recv_sem=recv,
            device_id=device, device_id_type=MESH,
        )

    def first_hop(s, da, db):
        i, j = lax.rem(a + da, A), lax.rem(b + db, B)
        if db:
            n = (db - 1) * A + da
            yield remote(par.at[s, 0, i, j], one_b.at[s, db - 1, i],
                         s1b.at[s, n], r1b.at[s, n], to_b(db))
        if da:
            n = (da - 1) * B + db
            yield remote(par.at[s, 1, i, j], one_a.at[s, da - 1, j],
                         s1a.at[s, n], r1a.at[s, n], to_a(da))

    def first_hops(s):
        for piece in pieces:
            yield from first_hop(s, *piece)

    def second_hops(s):
        for k in range(1, A):
            yield remote(mid_b.at[s, lax.rem(a + k, A)], two_b.at[s, k - 1],
                         s2b.at[s, k - 1], r2b.at[s, k - 1], to_a(k))
        for k in range(1, B):
            yield remote(mid_a.at[s, lax.rem(b + k, B)], two_a.at[s, k - 1],
                         s2a.at[s, k - 1], r2a.at[s, k - 1], to_b(k))

    def own_sends(s):
        for k in range(1, B):
            yield remote(gat.at[s, :, a, b], gat.at[s, :, a, b],
                         sgb.at[s, k - 1], rgb.at[s, k - 1], to_b(k))
        for k in range(1, A):
            yield remote(gat.at[s, :, a, b], gat.at[s, :, a, b],
                         sga.at[s, k - 1], rga.at[s, k - 1], to_a(k))

    def relays(s):
        for j in range(1, B):
            for k in range(1, A):
                block = gat.at[s, 0, a, lax.rem(b + j, B)]
                i = (j - 1) * (A - 1) + k - 1
                yield remote(block, block, srb.at[s, i], rrb.at[s, i], to_a(k))
        for j in range(1, A):
            for k in range(1, B):
                block = gat.at[s, 1, lax.rem(a + j, A), b]
                i = (j - 1) * (B - 1) + k - 1
                yield remote(block, block, sra.at[s, i], rra.at[s, i], to_b(k))

    def block_of(p):
        return lax.rem(a + pieces[p][0], A), lax.rem(b + pieces[p][1], B)

    def crossing(p):
        i, j = block_of(p)
        yield remote(part.at[i, j, 1 - core], cross.at[p], scx.at[p], rcx.at[p], partner)

    def scatters(p):
        for k in range(1, Z):
            yield remote(chip.at[p, lax.rem(z + k, Z)], terms.at[p, k - 1],
                         szr.at[p, k - 1], rzr.at[p, k - 1], to_z(k))

    def gathers(p):
        i, j = block_of(p)
        block = proj.at[i, j, core, z]
        for k in range(1, Z):
            yield remote(block, block, szg.at[p, k - 1], rzg.at[p, k - 1], to_z(k))

    def shares(p, first_k, last_k):
        i, j = block_of(p)
        for k in range(first_k, last_k):
            block = proj.at[i, j, core, lax.rem(z + k, Z)]
            yield remote(block, block, spg.at[p, k], rpg.at[p, k], partner)

    source = row
    far = jnp.abs(z - source)

    def upward(i):
        block = bas.at[core, i]
        return remote(block, block, sbu.at[i], rbc.at[i], {"col": lax.rem(z + 1, Z) * 2 + core})

    def downward(i):
        block = bas.at[core, i]
        return remote(block, block, sbd.at[i], rbc.at[i], {"col": lax.rem(z + Z - 1, Z) * 2 + core})

    def beside(i):
        block = bas.at[core, i]
        return remote(block, block, sbp.at[i], rbp.at[i], partner)

    goes_up = (z >= source) & (z < Z - 1)
    goes_down = (z <= source) & (z > 0)

    def spread_step(it):
        i = it - far

        @pl.when((i >= 0) & (i < chunks))
        def _():
            @pl.when(far > 0)
            def _():
                upward(i).wait_recv()

            @pl.when(goes_up)
            def _():
                upward(i).start()

            @pl.when(goes_down)
            def _():
                downward(i).start()

            beside(i).start()

    def result(s):
        return pltpu.make_async_copy(gat.at[s], gathered.at[s], out_sem.at[0, s])

    def every(body):
        lax.fori_loop(0, steps, lambda s, c: (body(s), c)[1], 0)

    own_basis = pltpu.make_async_copy(basis, bas.at[core], bas_in)

    @pl.when(far == 0)
    def _():
        own_basis.start()

    every(lambda s: [c.start() for c in loads(s)])

    barrier = pltpu.get_barrier_semaphore()
    for k in range(1, B):
        pl.semaphore_signal(barrier, inc=1, device_id=to_b(k), device_id_type=MESH)
    for k in range(1, A):
        pl.semaphore_signal(barrier, inc=1, device_id=to_a(k), device_id_type=MESH)
    for k in range(1, Z):
        pl.semaphore_signal(barrier, inc=1, device_id=to_z(k), device_id_type=MESH)
    pl.semaphore_signal(barrier, inc=1, device_id=partner, device_id_type=MESH)
    pl.semaphore_wait(barrier, A + B + Z - 2)

    f32, bf16 = jnp.float32, jnp.bfloat16
    count = len(pieces)
    for p in range(count):
        for c in crossing(p):
            c.start()

    def scatter(p):
        i, j = block_of(p)
        for c in crossing(p):
            c.wait_recv()
        chip[p] = (part[i, j, core].astype(f32) + cross[p].astype(f32)).astype(bf16)
        for c in scatters(p):
            c.start()

    scatter(0)
    for p in range(count):
        i, j = block_of(p)
        for c in scatters(p):
            c.wait_recv()
        total = chip[p, z].astype(f32)
        for k in range(Z - 1):
            total += terms[p, k].astype(f32)
        proj[i, j, core, z] = total.astype(bf16)
        for c in gathers(p):
            c.start()
        for c in shares(p, 0, 1):
            c.start()
        if p + 1 < count:
            scatter(p + 1)
        for c in gathers(p):
            c.wait_recv()
        for c in shares(p, 1, Z):
            c.start()
        for c in shares(p, 0, Z):
            c.wait_recv()

        def partial_step(s, carry, p=p, i=i, j=j):
            if p == 0:
                loads(s)[0].wait()
            got = jnp.dot(proj[i, j].reshape(rb, -1), hid[s], preferred_element_type=f32)
            par[s, 0, i, j] = got[:, :W].astype(bf16)
            par[s, 1, i, j] = got[:, W:].astype(bf16)
            for c in first_hop(s, *pieces[p]):
                c.start()
            return carry

        lax.fori_loop(0, steps, partial_step, 0)

    @pl.when(far == 0)
    def _():
        own_basis.wait()

    def turn(it, carry):
        spread_step(it)

        @pl.when(it < steps)
        def _():
            s = it
            for c in first_hops(s):
                c.wait_recv()
            for i in range(A):
                total = par[s, 0, i, b].astype(f32)
                for k in range(B - 1):
                    total += one_b[s, k, i].astype(f32)
                mid_b[s, i] = total.astype(jnp.bfloat16)
            for i in range(B):
                total = par[s, 1, a, i].astype(f32)
                for k in range(A - 1):
                    total += one_a[s, k, i].astype(f32)
                mid_a[s, i] = total.astype(jnp.bfloat16)
            for c in second_hops(s):
                c.start()

        @pl.when((it >= 1) & (it < steps + 1))
        def _():
            s = it - 1
            for c in second_hops(s):
                c.wait_recv()
            for c in loads(s)[1:]:
                c.wait()
            for t in range(2):
                if t == 0:
                    gradient = mid_b[s, a].astype(f32)
                    for k in range(A - 1):
                        gradient += two_b[s, k].astype(f32)
                else:
                    gradient = mid_a[s, b].astype(f32)
                    for k in range(B - 1):
                        gradient += two_a[s, k].astype(f32)
                cols = slice(t * W, (t + 1) * W)
                one = beta_one * mom_one[s, :, cols] + (1.0 - beta_one) * gradient
                two = beta_two * mom_two[s, :, cols] + (1.0 - beta_two) * gradient * gradient
                first_hat = one / (1.0 - beta_one**STEP_COUNT)
                second_hat = two / (1.0 - beta_two**STEP_COUNT)
                gat[s, t, a, b] = (first_hat / (jnp.sqrt(second_hat) + epsilon)).astype(jnp.bfloat16)
                mom_one[s, :, cols] = one
                mom_two[s, :, cols] = two
            for c in own_sends(s):
                c.start()
            for c in stores(s):
                c.start()

        @pl.when((it >= 2) & (it < steps + 2))
        def _():
            s = it - 2
            for c in own_sends(s):
                c.wait_recv()
            for c in relays(s):
                c.start()

        @pl.when((it >= 3) & (it < steps + 3))
        def _():
            s = it - 3
            for c in relays(s):
                c.wait_recv()
            result(s).start()

        return carry

    lax.fori_loop(0, max(steps + 3, chunks + Z - 1), turn, 0)

    def finish_basis(i, carry):
        beside(i).wait()

        @pl.when(goes_up)
        def _():
            upward(i).wait_send()

        @pl.when(goes_down)
        def _():
            downward(i).wait_send()

        return carry

    lax.fori_loop(0, chunks, finish_basis, 0)
    spread_out = pltpu.make_async_copy(bas, spread, bas_out)
    spread_out.start()
    for p in range(count):
        for group in (crossing(p), scatters(p), gathers(p), shares(p, 0, Z)):
            for c in group:
                c.wait_send()

    def finish(s):
        for group in (first_hops, second_hops, own_sends, relays):
            for c in group(s):
                c.wait_send()
        for c in stores(s):
            c.wait()
        result(s).wait()

    every(finish)
    spread_out.wait()


def row_part(rows, banks, part, hidden, first, second, basis):
    Z = banks // 2
    B = 2 if rows % 2 == 0 else 1
    A = rows // B
    rank, tokens = part.shape
    rb, cols = first.shape
    rk = rb // banks
    count = rows
    chunks = 8
    depth = basis.shape[0] // chunks
    part = part.reshape(A, B, 2, Z, rk, tokens)
    basis = basis.reshape(chunks, depth, rank)
    W = 256 if cols % 512 == 0 else 128
    steps = cols // (2 * W)
    bf16, f32 = jnp.bfloat16, jnp.float32
    nb, na = max(B - 1, 1), max(A - 1, 1)
    nr = na * nb

    def pair(n):
        return [pltpu.SemaphoreType.DMA((steps, n)), pltpu.SemaphoreType.DMA((steps, n))]

    def two(*shape):
        return [pltpu.SemaphoreType.DMA(shape), pltpu.SemaphoreType.DMA(shape)]

    one = pltpu.SemaphoreType.DMA((chunks,))

    anywhere = pl.BlockSpec(memory_space=pl.ANY)
    return pl.pallas_call(
        functools.partial(row_kernel, A, B, Z, steps, rb, W, chunks),
        name="row_part",
        out_shape=(
            jax.ShapeDtypeStruct((steps, 2, A, B, rb, W), bf16),
            jax.ShapeDtypeStruct(first.shape, f32),
            jax.ShapeDtypeStruct(second.shape, f32),
            jax.ShapeDtypeStruct((2,) + basis.shape, bf16),
        ),
        in_specs=[pl.BlockSpec(memory_space=pltpu.VMEM)] + [anywhere] * 4,
        out_specs=(anywhere,) * 4,
        scratch_shapes=[
            pltpu.VMEM((count, Z, rk, tokens), bf16),
            pltpu.VMEM((count, Z, rk, tokens), bf16),
            pltpu.VMEM((count, Z - 1, rk, tokens), bf16),
            pltpu.VMEM((A, B, 2, Z, rk, tokens), bf16),
            pltpu.VMEM((2,) + basis.shape, bf16),
            pltpu.VMEM((steps, tokens, 2 * W), bf16),
            pltpu.VMEM((steps, 2, A, B, rb, W), bf16),
            pltpu.VMEM((steps, nb, A, rb, W), bf16),
            pltpu.VMEM((steps, na, B, rb, W), bf16),
            pltpu.VMEM((steps, A, rb, W), bf16),
            pltpu.VMEM((steps, B, rb, W), bf16),
            pltpu.VMEM((steps, na, rb, W), bf16),
            pltpu.VMEM((steps, nb, rb, W), bf16),
            pltpu.VMEM((steps, 2, A, B, rb, W), bf16),
            pltpu.VMEM((steps, rb, 2 * W), f32),
            pltpu.VMEM((steps, rb, 2 * W), f32),
            pltpu.SemaphoreType.DMA((3, steps)),
            pltpu.SemaphoreType.DMA((3, steps)),
        ] + pair(nb * A) + pair(na * B) + pair(na) + pair(nb) + pair(nb) + pair(na) + pair(nr) + pair(nr)
        + two(count) + two(count, Z - 1) + two(count, Z - 1) + two(count, Z)
        + [one] * 5 + [pltpu.SemaphoreType.DMA, pltpu.SemaphoreType.DMA],
        compiler_params=pltpu.CompilerParams(
            collective_id=0, has_side_effects=True, vmem_limit_bytes=60 << 20
        ),
        cost_estimate=pl.CostEstimate(
            flops=2 * rank * tokens * cols * 8, bytes_accessed=400 << 20, transcendentals=0
        ),
    )(part, hidden, first, second, basis)


def update_kernel(W, basis, direction, weight, first, second, out, first_out, second_out):
    first_out[...] = first[...]
    second_out[...] = second[...]
    for t in range(2):
        cols = slice(t * W, (t + 1) * W)
        update = jnp.dot(basis[...], direction[0, t], preferred_element_type=jnp.float32)
        out[:, cols] = (weight[:, cols].astype(jnp.float32) - step_size * update).astype(jnp.bfloat16)


def apply_update(basis, gathered, weight, first, second):
    steps, _, rank, W = gathered.shape
    rows, cols = weight.shape
    wide = pl.BlockSpec((rows, 2 * W), lambda j: (0, j))
    moment = pl.BlockSpec((first.shape[0], 2 * W), lambda j: (0, j))
    return pl.pallas_call(
        functools.partial(update_kernel, W),
        name="apply_update",
        out_shape=tuple(jax.ShapeDtypeStruct(x.shape, x.dtype) for x in (weight, first, second)),
        grid=(steps,),
        in_specs=[
            pl.BlockSpec((rows, rank), lambda j: (0, 0), pipeline_mode=pl.Buffered(1)),
            pl.BlockSpec((1, 2, rank, W), lambda j: (j, 0, 0, 0)),
            wide, moment, moment,
        ],
        out_specs=(wide, moment, moment),
        compiler_params=pltpu.CompilerParams(
            dimension_semantics=("arbitrary",), vmem_limit_bytes=56 << 20
        ),
        cost_estimate=pl.CostEstimate(
            flops=2 * rank * rows * cols, bytes_accessed=3 * weight.size * 2, transcendentals=0
        ),
    )(basis, gathered, weight, first, second)


def local(rows, banks, out_grad, hidden, basis, weight, first_moment, second_moment):
    part = lax.dot_general(
        basis, out_grad, (((0,), (1,)), ((), ())), preferred_element_type=jnp.float32
    ).astype(jnp.bfloat16)
    gathered, new_first, new_second, spread = row_part(
        rows, banks, part, hidden, first_moment, second_moment, basis
    )
    steps, W = gathered.shape[0], gathered.shape[-1]
    gathered = gathered.reshape(steps, 2, -1, W)
    return apply_update(
        spread.reshape(-1, basis.shape[1]), gathered, weight, new_first, new_second
    )


def solution(mesh):
    in_specs = (
        P("row", "col"),
        P("row", "col"),
        P("col", None),
        P("row", "col"),
        P("row", "col"),
        P("row", "col"),
    )
    out_specs = (P("row", "col"), P("row", "col"), P("row", "col"))
    return jax.shard_map(
        functools.partial(local, mesh.shape["row"], mesh.shape["col"]),
        mesh=mesh, in_specs=in_specs, out_specs=out_specs, check_vma=False,
    )
```
